32 devices in a mesh: dom: 32 (over z, y, x, core).
Axes of the slice: x: 2, y: 2, z: 4, core: 2. Of those that a mesh axis runs over, the one named last changes fastest.
Arguments:
- feats: bfloat16 [131072, 512], P('dom'), may hold values from -6 to 6
- w_self: bfloat16 [512, 512], replicated, may hold values from -0.25 to 0.25
- w_neigh: bfloat16 [512, 512], replicated, may hold values from -0.25 to 0.25
- bias: float32 [512], replicated, may hold values from -1 to 1
- local_tiles: bfloat16 [1024, 3, 128, 128], P('dom'), may hold values from -0.15625 to 0.15625
- local_src: int32 [1024, 3], P('dom'), may hold values from 0 to 31
- local_cnt: int32 [1024], P('dom'), may hold values from 1 to 3
- halo_send: int32 [32, 32], P('dom'), may hold values from 0 to 31
- halo_dst: int32 [32, 32], P('dom'), may hold values from 0 to 31
- halo_tiles: bfloat16 [32, 32, 128, 128], P('dom'), may hold values from -0.15625 to 0.15625
- push_src: int32 [32, 32], P('dom'), may hold values from 0 to 31
- push_dst: int32 [32, 32], P('dom'), may hold values from 0 to 31
- push_tiles: bfloat16 [32, 32, 128, 128], P('dom'), may hold values from -0.15625 to 0.15625
- cotangent: bfloat16 [131072, 512], P('dom'), may hold values from -6 to 6
Outputs:
- hidden_out: bfloat16 [131072, 512], P('dom')
- grad_self: float32 [512, 512], replicated
- grad_neigh: float32 [512, 512], replicated
- grad_bias: float32 [512], replicated
The draws below stay inside these ranges and needn't reach their ends.
All inputs are finite; a program needn't handle non-finite values.
Results may differ from the reference program's by a relative error of at most 0.007.
Values may be sent and summed in bfloat16 or wider, within the bound.
A program may use at most 320 MiB of HBM per device.

```python
import jax
import jax.numpy as jnp
from jax import lax

H = 512
BLK = 128
NB = 32
LPB = 3
NODES = 131072
N_DOM = 32


def place_ends(result, rng, least, largest):
    shape = result.shape
    place = [jax.random.randint(jax.random.fold_in(rng, axis), (), 0, shape[axis]) for axis in range(len(shape))]
    result = result.at[tuple(place)].set(least)
    longest = shape.index(max(shape))
    place[longest] = (place[longest] + 1) % shape[longest]
    return result.at[tuple(place)].set(largest)


def block_scale(stream_key, extent, shards, least, largest):
    gain, own = 1.0, jax.random.fold_in(stream_key, 6)
    for dim, shards_of in shards:
        draws = jnp.exp(jax.random.uniform(jax.random.fold_in(own, dim), (shards_of,), jnp.float32, least / len(shards), largest / len(shards)))
        gain = gain * jnp.repeat(draws, extent[dim] // shards_of).reshape([-1 if axis == dim else 1 for axis in range(len(extent))])
    return gain


def gaussian(key, extent, deviation, bound, pieces=(), kind=jnp.bfloat16):
    result = jax.random.normal(key, extent, jnp.float32) * deviation
    if len(pieces) > 0:
        result = block_scale(key, extent, pieces, -0.22, 0.18) * result
    return jnp.clip(result, min=-bound, max=bound).astype(kind)


def setup_inputs(seed: int = 0) -> dict:
    seeds = jax.random.split(jax.random.key(seed), 15)
    feats = gaussian(seeds[0], (NODES, H), 1.0, 6.0, ((0, 32),))
    w_self = gaussian(seeds[1], (H, H), H ** -0.5, 0.25)
    w_neigh = gaussian(seeds[2], (H, H), H ** -0.5, 0.25)
    bias = jnp.clip(jax.random.uniform(seeds[3], (H,), jnp.float32, -1.0, 1.0), -1.0, 1.0)
    local_tiles = gaussian(seeds[4], (NB * N_DOM, LPB, BLK, BLK), (BLK * 10) ** -0.5, 0.15625, ((0, 32),))
    local_src = place_ends(jax.random.randint(seeds[5], (NB * N_DOM, LPB), 0, NB), jax.random.fold_in(seeds[5], 1), 0, NB - 1).astype(jnp.int32)
    local_cnt = place_ends(jax.random.randint(seeds[6], (NB * N_DOM,), 1, LPB + 1), jax.random.fold_in(seeds[6], 1), 1, LPB).astype(jnp.int32)
    halo_send = place_ends(jax.random.randint(seeds[7], (N_DOM, N_DOM), 0, NB), jax.random.fold_in(seeds[7], 1), 0, NB - 1).astype(jnp.int32)
    halo_dst = place_ends(jax.random.randint(seeds[8], (N_DOM, N_DOM), 0, NB), jax.random.fold_in(seeds[8], 1), 0, NB - 1).astype(jnp.int32)
    halo_tiles = gaussian(seeds[9], (N_DOM, N_DOM, BLK, BLK), (BLK * 10) ** -0.5, 0.15625, ((0, 32),))
    push_src = place_ends(jax.random.randint(seeds[10], (N_DOM, N_DOM), 0, NB), jax.random.fold_in(seeds[10], 1), 0, NB - 1).astype(jnp.int32)
    push_dst = place_ends(jax.random.randint(seeds[11], (N_DOM, N_DOM), 0, NB), jax.random.fold_in(seeds[11], 1), 0, NB - 1).astype(jnp.int32)
    push_tiles = gaussian(seeds[12], (N_DOM, N_DOM, BLK, BLK), (BLK * 10) ** -0.5, 0.15625, ((0, 32),))
    cotangent = gaussian(seeds[13], (NODES, H), 1.0, 6.0, ((0, 32),))
    return {"feats": feats, "w_self": w_self, "w_neigh": w_neigh, "bias": bias, "local_tiles": local_tiles, "local_src": local_src, "local_cnt": local_cnt, "halo_send": halo_send, "halo_dst": halo_dst, "halo_tiles": halo_tiles, "push_src": push_src, "push_dst": push_dst, "push_tiles": push_tiles, "cotangent": cotangent}


def reference(feats, w_self, w_neigh, bias, local_tiles, local_src, local_cnt, halo_send, halo_dst, halo_tiles, push_src, push_dst, push_tiles, cotangent):
    blocks = feats.reshape(N_DOM, NB, BLK, H)
    tiles_all = local_tiles.reshape(N_DOM, NB, LPB, BLK, BLK)
    source_all = local_src.reshape(N_DOM, NB, LPB)
    count_all = local_cnt.reshape(N_DOM, NB)
    owner_ids = jnp.arange(N_DOM)
    slot_ids = jnp.arange(LPB)

    def one_part(part_id):
        own_blocks = blocks[part_id]
        gathered = own_blocks[source_all[part_id]]
        keep_mask = (slot_ids[None, :] < count_all[part_id][:, None]).astype(jnp.bfloat16)
        masked = tiles_all[part_id] * keep_mask[:, :, None, None]
        agg_sum = jnp.einsum('bjik,bjkh->bih', masked.astype(jnp.float32), gathered.astype(jnp.float32))
        halo_in = blocks[owner_ids, halo_send[:, part_id]]
        halo_part = jnp.einsum('qik,qkh->qih', halo_tiles[part_id].astype(jnp.float32), halo_in.astype(jnp.float32))
        agg_sum = agg_sum.at[halo_dst[part_id]].add(halo_part)
        push_in = blocks[owner_ids, push_src[:, part_id]]
        pushed = jnp.einsum('sik,skh->sih', push_tiles[:, part_id].astype(jnp.float32), push_in.astype(jnp.float32)).astype(jnp.bfloat16)
        pushed = lax.optimization_barrier(pushed).astype(jnp.float32)
        agg_sum = agg_sum.at[push_dst[:, part_id]].add(pushed)
        return agg_sum.astype(jnp.bfloat16)

    agg = lax.map(one_part, jnp.arange(N_DOM)).reshape(NODES, H)
    pre = jnp.dot(feats, w_self, preferred_element_type=jnp.float32) + jnp.dot(agg, w_neigh, preferred_element_type=jnp.float32) + bias
    sigma = jax.nn.sigmoid(pre)
    hidden_out = (pre * sigma).astype(jnp.bfloat16)
    dpre = (cotangent.astype(jnp.float32) * sigma * (1.0 + pre * (1.0 - sigma))).astype(jnp.bfloat16)
    grad_self = jnp.dot(feats.T, dpre, preferred_element_type=jnp.float32)
    grad_neigh = jnp.dot(agg.T, dpre, preferred_element_type=jnp.float32)
    grad_bias = jnp.sum(dpre.astype(jnp.float32), axis=0)
    return hidden_out, grad_self, grad_neigh, grad_bias
```

```python
import functools

import jax
import jax.numpy as jnp
from jax import lax
from jax.experimental import pallas as pl
from jax.experimental.pallas import tpu as pltpu
from jax.sharding import PartitionSpec as P

MESH = pl.DeviceIdType.MESH
VMEM_BYTES = 66_000_000
PLANE = 8


def flip(me, mask, n):
    out = 0
    weight = 1
    while weight < n:
        out = out + weight * ((me // weight + mask // weight) % 2)
        weight *= 2
    return out


def greet_all(n, me):
    barrier = pltpu.get_barrier_semaphore()

    def greet(i, carry):
        pl.semaphore_signal(
            barrier, inc=1, device_id=(lax.rem(me + i, n),), device_id_type=MESH
        )
        return carry

    lax.fori_loop(1, n, greet, 0)
    return barrier


def exchange_kernel(
    n,
    send_ids,
    push_ids,
    local_ids,
    keep,
    feats,
    push_tiles,
    local_tiles,
    w_self,
    bias,
    dst_rows,
    halo_in,
    push_in,
    dst_in,
    local_out,
    base_out,
    halo_buf,
    push_buf,
    local_buf,
    base_buf,
    halo_ss,
    halo_rs,
    push_ss,
    push_rs,
    dst_ss,
    dst_rs,
    own_sems,
    out_sems,
):
    me = lax.axis_index("dom")
    blk = push_tiles.shape[1]
    planes = n // PLANE
    barrier = greet_all(n, me)

    def message(i):
        mask = ((i % planes + 1) % planes) * PLANE + i // planes
        return mask, flip(me, mask, n)

    def gather(i, carry):
        _, to = message(i)
        halo_buf[to] = feats[send_ids[0, to]]
        return carry

    lax.fori_loop(0, n, gather, 0)
    pl.semaphore_wait(barrier, n - 1)

    def halo_copy(to):
        return pltpu.make_async_remote_copy(
            halo_buf.at[to], halo_in.at[me], halo_ss, halo_rs, device_id=(to,), device_id_type=MESH
        )

    def push_copy(to):
        return pltpu.make_async_remote_copy(
            push_buf.at[to], push_in.at[me], push_ss, push_rs, device_id=(to,), device_id_type=MESH
        )

    def dst_copy(to):
        return pltpu.make_async_remote_copy(
            dst_rows.at[to], dst_in.at[me], dst_ss, dst_rs, device_id=(to,), device_id_type=MESH
        )

    def first(i, carry):
        mask, to = message(i)

        @pl.when(mask > 0)
        def _():
            halo_copy(to).start()
            dst_copy(to).start()

        push_buf[to] = jnp.dot(
            push_tiles[to], feats[push_ids[0, to]], preferred_element_type=jnp.float32
        ).astype(jnp.bfloat16)
        return carry

    lax.fori_loop(0, n, first, 0)

    def second(i, carry):
        mask, to = message(i)

        @pl.when(mask > 0)
        def _():
            push_copy(to).start()

        return carry

    lax.fori_loop(0, n, second, 0)
    own = (
        pltpu.make_async_copy(halo_buf.at[me], halo_in.at[me], own_sems.at[0]),
        pltpu.make_async_copy(push_buf.at[me], push_in.at[me], own_sems.at[1]),
        pltpu.make_async_copy(dst_rows.at[me], dst_in.at[me], own_sems.at[2]),
    )
    for copy in own:
        copy.start()

    slots = local_tiles.shape[1]

    def local(b, carry):
        total = jnp.zeros(feats.shape[1:], jnp.float32)
        for j in range(slots):
            tile = local_tiles[b, j] * keep[b * slots + j].astype(jnp.bfloat16)
            total += jnp.dot(tile, feats[local_ids[b, j]], preferred_element_type=jnp.float32)
        rows = pl.ds(pl.multiple_of(b * blk, blk), blk)
        local_buf[rows, :] = total
        base_buf[rows, :] = (
            jnp.dot(feats[b], w_self[...], preferred_element_type=jnp.float32) + bias[...]
        )
        return carry

    lax.fori_loop(0, feats.shape[0], local, 0)
    outs = (
        pltpu.make_async_copy(local_buf, local_out, out_sems.at[0]),
        pltpu.make_async_copy(base_buf, base_out, out_sems.at[1]),
    )
    for copy in outs:
        copy.start()
    for copy in own + outs:
        copy.wait()
    for buf, sem in (
        (halo_in, halo_rs),
        (push_in, push_rs),
        (dst_in, dst_rs),
        (halo_buf, halo_ss),
        (push_buf, push_ss),
        (dst_rows, dst_ss),
    ):
        part = buf.at[pl.ds(0, n - 1)]
        pltpu.make_async_copy(part, part, sem).wait()


def exchange(n, send_ids, push_ids, local_ids, keep, feats, push_tiles, local_tiles, w_self, bias, dst_rows):
    blocks, blk, width = feats.shape
    smem = pl.BlockSpec(memory_space=pltpu.SMEM)
    vmem = pl.BlockSpec(memory_space=pltpu.VMEM)
    hbm = pl.BlockSpec(memory_space=pl.ANY)
    dma = pltpu.SemaphoreType.DMA
    return pl.pallas_call(
        functools.partial(exchange_kernel, n),
        out_shape=(
            jax.ShapeDtypeStruct((n, blk, width), jnp.bfloat16),
            jax.ShapeDtypeStruct((n, blk, width), jnp.bfloat16),
            jax.ShapeDtypeStruct(dst_rows.shape, jnp.int32),
            jax.ShapeDtypeStruct((blocks * blk, width), jnp.float32),
            jax.ShapeDtypeStruct((blocks * blk, width), jnp.float32),
        ),
        in_specs=[smem] * 3 + [vmem] * 7,
        out_specs=(hbm,) * 5,
        scratch_shapes=[
            pltpu.VMEM((n, blk, width), jnp.bfloat16),
            pltpu.VMEM((n, blk, width), jnp.bfloat16),
            pltpu.VMEM((blocks * blk, width), jnp.float32),
            pltpu.VMEM((blocks * blk, width), jnp.float32),
        ]
        + [dma] * 6
        + [dma((3,)), dma((2,))],
        compiler_params=pltpu.CompilerParams(
            collective_id=0, has_side_effects=True, vmem_limit_bytes=VMEM_BYTES
        ),
        name="exchange",
    )(send_ids, push_ids, local_ids, keep, feats, push_tiles, local_tiles, w_self, bias, dst_rows)


def dense_kernel(
    steps,
    group,
    halo_dst,
    push_dst,
    halo_in,
    halo_tiles,
    push_in,
    local_part,
    base,
    feats,
    cot,
    w_neigh,
    hidden,
    grads,
    gbias,
    acc,
    gt,
    gb,
):
    i = pl.program_id(0)
    blk = halo_in.shape[1]
    rows, width = feats.shape

    @pl.when(i == 0)
    def _():
        acc[...] = jnp.zeros_like(acc)
        gt[...] = jnp.zeros_like(gt)
        gb[...] = jnp.zeros_like(gb)

    @pl.when(i < steps)
    def _():
        for k in range(group):
            q = i * group + k
            at = pl.ds(pl.multiple_of(halo_dst[q] * blk, blk), blk)
            acc[at, :] += jnp.dot(halo_tiles[k], halo_in[k], preferred_element_type=jnp.float32)
            at = pl.ds(pl.multiple_of(push_dst[q] * blk, blk), blk)
            acc[at, :] += push_in[k].astype(jnp.float32)

    @pl.when(i >= steps)
    def _():
        at = pl.ds(pl.multiple_of((i - steps) * rows, rows), rows)
        agg = (acc[at, :] + local_part[...]).astype(jnp.bfloat16)
        pre = base[...] + jnp.dot(agg, w_neigh[...], preferred_element_type=jnp.float32)
        sigma = jax.nn.sigmoid(pre)
        hidden[...] = (pre * sigma).astype(jnp.bfloat16)
        dpre = (cot[...].astype(jnp.float32) * sigma * (1.0 + pre * (1.0 - sigma))).astype(
            jnp.bfloat16
        )
        gb[...] += jnp.sum(dpre.astype(jnp.float32).reshape(rows // 8, 8, width), axis=0)
        turned = dpre.T
        gt[0] += jnp.dot(turned, feats[...], preferred_element_type=jnp.float32)
        gt[1] += jnp.dot(turned, agg, preferred_element_type=jnp.float32)

    @pl.when(i == pl.num_programs(0) - 1)
    def _():
        grads[pl.ds(0, width), :] = gt[0].T
        grads[pl.ds(width, width), :] = gt[1].T
        gbias[...] = jnp.broadcast_to(jnp.sum(gb[...], axis=0, keepdims=True), gbias.shape)


def dense(halo_dst, push_dst, halo_in, halo_tiles, push_in, local_part, base, feats, cot, w_neigh):
    n, blk, width = halo_in.shape
    nodes = feats.shape[0]
    group, rows = 4, 512
    steps, chunks = n // group, nodes // rows

    def owners(i, *_):
        return (jnp.minimum(i, steps - 1), 0, 0)

    def nodes_at(i, *_):
        return (jnp.maximum(i - steps, 0), 0)

    arrived = pl.BlockSpec((group, blk, width), owners)
    chunk = pl.BlockSpec((rows, width), nodes_at)

    def whole(i, *_):
        return (0, 0)

    return pl.pallas_call(
        functools.partial(dense_kernel, steps, group),
        out_shape=(
            jax.ShapeDtypeStruct((nodes, width), jnp.bfloat16),
            jax.ShapeDtypeStruct((2 * width, width), jnp.float32),
            jax.ShapeDtypeStruct((8, width), jnp.float32),
        ),
        grid_spec=pltpu.PrefetchScalarGridSpec(
            num_scalar_prefetch=2,
            grid=(steps + chunks,),
            in_specs=[
                arrived,
                pl.BlockSpec((group, blk, blk), owners),
                arrived,
                chunk,
                chunk,
                chunk,
                chunk,
                pl.BlockSpec((width, width), whole),
            ],
            out_specs=(
                chunk,
                pl.BlockSpec((2 * width, width), whole),
                pl.BlockSpec((8, width), whole),
            ),
            scratch_shapes=[
                pltpu.VMEM((nodes, width), jnp.float32),
                pltpu.VMEM((2, width, width), jnp.float32),
                pltpu.VMEM((8, width), jnp.float32),
            ],
        ),
        compiler_params=pltpu.CompilerParams(
            dimension_semantics=("arbitrary",), vmem_limit_bytes=VMEM_BYTES
        ),
        name="dense",
    )(halo_dst, push_dst, halo_in, halo_tiles, push_in, local_part, base, feats, cot, w_neigh)


def reduce_kernel(
    n, term, gbias, out, bias_out, acc, send_buf, recv_buf, bias_in, ss, rs, gs, gr, bs, br, own
):
    me = lax.axis_index("dom")
    barrier = greet_all(n, me)
    size = term.shape[0]
    core, second, third = me % 2, (me // 2) % 2, (me // 4) % 2
    bits = [core, second * (1 - core) + third * core, third * (1 - core) + second * core]
    weights = [1, 2 + 2 * core, 4 - 2 * core]
    weight = 8
    while weight < n:
        bits.append((me // weight) % 2)
        weights.append(weight)
        weight *= 2
    partners = [me + (1 - 2 * bit) * w for bit, w in zip(bits, weights)]

    def bias_copy(to):
        return pltpu.make_async_remote_copy(
            gbias, bias_in.at[me], bs, br, device_id=(to,), device_id_type=MESH
        )

    own_bias = pltpu.make_async_copy(gbias, bias_in.at[me], own)
    own_bias.start()
    half = size // 2
    away = pl.multiple_of((1 - bits[0]) * half, half)
    send_buf[pl.ds(0, half), :] = term[pl.ds(away, half), :].astype(jnp.bfloat16)
    pl.semaphore_wait(barrier, n - 1)

    base = 0
    lo = 0
    for step, (bit, partner) in enumerate(zip(bits, partners)):
        half = size // 2
        copy = pltpu.make_async_remote_copy(
            send_buf.at[pl.ds(base, half)],
            recv_buf.at[pl.ds(base, half)],
            ss.at[step],
            rs.at[step],
            device_id=(partner,),
            device_id_type=MESH,
        )
        copy.start()
        if step == 0:

            def greet(i, carry):
                bias_copy(lax.rem(me + i, n)).start()
                return carry

            lax.fori_loop(1, n, greet, 0)
        lo = lo + bit * half
        source = term if step == 0 else acc
        copy.wait()
        if step + 1 < len(bits):
            nxt = half // 2
            bit2 = bits[step + 1]
            away = (1 - bit2) * nxt
            at = pl.multiple_of(lo + away, nxt)
            rel = pl.multiple_of(away, nxt)
            send_buf[pl.ds(base + half, nxt), :] = (
                source[pl.ds(at, nxt), :]
                + recv_buf[pl.ds(pl.multiple_of(base + rel, nxt), nxt), :].astype(jnp.float32)
            ).astype(jnp.bfloat16)
            keep = bit2 * nxt
            at = pl.multiple_of(lo + keep, nxt)
            acc[pl.ds(at, nxt), :] = source[pl.ds(at, nxt), :] + recv_buf[
                pl.ds(pl.multiple_of(base + keep, nxt), nxt), :
            ].astype(jnp.float32)
        else:
            at = pl.multiple_of(lo, half)
            out[pl.ds(at, half), :] = (
                source[pl.ds(at, half), :] + recv_buf[pl.ds(base, half), :].astype(jnp.float32)
            ).astype(jnp.bfloat16)
        base += half
        size = half

    own_bias.wait()
    part = bias_in.at[pl.ds(0, n - 1)]
    pltpu.make_async_copy(part, part, br).wait()
    bias_out[...] = jnp.sum(bias_in[...], axis=0)

    for step in reversed(range(len(bits))):
        at = pl.ds(pl.multiple_of(lo, size), size)
        copy = pltpu.make_async_remote_copy(
            out.at[at],
            out.at[at],
            gs.at[step],
            gr.at[step],
            device_id=(partners[step],),
            device_id_type=MESH,
        )
        copy.start()
        copy.wait()
        lo = lo - bits[step] * size
        size *= 2
    part = bias_in.at[pl.ds(0, n - 1)]
    pltpu.make_async_copy(part, part, bs).wait()


def reduce(n, term, gbias):
    size, width = term.shape
    steps = n.bit_length() - 1
    vmem = pl.BlockSpec(memory_space=pltpu.VMEM)
    dma = pltpu.SemaphoreType.DMA
    return pl.pallas_call(
        functools.partial(reduce_kernel, n),
        out_shape=(
            jax.ShapeDtypeStruct((size, width), jnp.bfloat16),
            jax.ShapeDtypeStruct(gbias.shape, jnp.float32),
        ),
        in_specs=[vmem, vmem],
        out_specs=(vmem, vmem),
        scratch_shapes=[
            pltpu.VMEM((size, width), jnp.float32),
            pltpu.VMEM((size, width), jnp.bfloat16),
            pltpu.VMEM((size, width), jnp.bfloat16),
            pltpu.VMEM((n,) + gbias.shape, jnp.float32),
            dma((steps,)),
            dma((steps,)),
            dma((steps,)),
            dma((steps,)),
            dma,
            dma,
            dma,
        ],
        compiler_params=pltpu.CompilerParams(
            collective_id=1, has_side_effects=True, vmem_limit_bytes=VMEM_BYTES
        ),
        name="reduce_grads",
    )(term, gbias)


def shards(
    n,
    feats,
    w_self,
    w_neigh,
    bias,
    local_tiles,
    local_src,
    local_cnt,
    halo_send,
    halo_dst,
    halo_tiles,
    push_src,
    push_dst,
    push_tiles,
    cotangent,
):
    width = feats.shape[1]
    live = jnp.arange(local_tiles.shape[1])[None, :] < local_cnt[:, None]
    keep = jnp.broadcast_to(live.astype(jnp.float32).reshape(-1, 1, 1), (live.size, 1, 128))
    dst_rows = jnp.broadcast_to(push_dst[0][:, None, None], (n, 8, 128))
    halo_in, push_in, dst_in, local_part, base = exchange(
        n,
        halo_send,
        push_src,
        local_src,
        keep,
        feats.reshape(-1, push_tiles.shape[2], width),
        push_tiles[0],
        local_tiles,
        w_self,
        bias[None, :],
        dst_rows,
    )
    hidden_out, term, term_bias = dense(
        halo_dst[0],
        dst_in[:, 0, 0],
        halo_in,
        halo_tiles[0],
        push_in,
        local_part,
        base,
        feats,
        cotangent,
        w_neigh,
    )
    grads, gbias = reduce(n, term, term_bias)
    grads = grads.astype(jnp.float32)
    return (hidden_out, grads[:width], grads[width:], gbias[0])


def solution(mesh):
    placed = (
        P("dom", None),
        P(),
        P(),
        P(),
        P("dom", None, None, None),
        P("dom", None),
        P("dom"),
        P("dom", None),
        P("dom", None),
        P("dom", None, None, None),
        P("dom", None),
        P("dom", None),
        P("dom", None, None, None),
        P("dom", None),
    )
    return jax.shard_map(
        functools.partial(shards, mesh.shape["dom"]),
        mesh=mesh,
        in_specs=placed,
        out_specs=(P("dom", None), P(), P(), P()),
        check_vma=False,
    )
```

```python
import functools

import jax
import jax.numpy as jnp
from jax import lax
from jax.experimental import pallas as pl
from jax.experimental.pallas import tpu as pltpu
from jax.sharding import PartitionSpec as P

MESH = pl.DeviceIdType.MESH
VMEM_BYTES = 66_000_000
PLANE = 8


def flip(me, mask, n):
    out = 0
    weight = 1
    while weight < n:
        out = out + weight * ((me // weight + mask // weight) % 2)
        weight *= 2
    return out


def greet_all(n, me):
    barrier = pltpu.get_barrier_semaphore()

    def greet(i, carry):
        pl.semaphore_signal(
            barrier, inc=1, device_id=(lax.rem(me + i, n),), device_id_type=MESH
        )
        return carry

    lax.fori_loop(1, n, greet, 0)
    return barrier


def exchange_kernel(
    n,
    send_ids,
    push_ids,
    local_ids,
    local_cnt,
    feats,
    push_tiles,
    local_tiles,
    w_self,
    bias,
    push_dst,
    halo_in,
    push_in,
    dst_in,
    local_out,
    base_out,
    halo_buf,
    push_buf,
    local_buf,
    base_buf,
    dst_buf,
    tile_buf,
    halo_ss,
    halo_rs,
    push_ss,
    push_rs,
    dst_ss,
    dst_rs,
    own_sems,
    out_sems,
):
    me = lax.axis_index("dom")
    blk = push_tiles.shape[1]
    planes = n // PLANE
    barrier = greet_all(n, me)
    load_tiles = pltpu.make_async_copy(local_tiles, tile_buf, out_sems.at[2])
    load_tiles.start()
    dst_buf[...] = jnp.zeros_like(dst_buf)
    dst_buf[:, pl.ds(0, n)] = push_dst[...]

    def message(i):
        mask = ((i % planes + 1) % planes) * PLANE + i // planes
        return mask, flip(me, mask, n)

    def gather(i, carry):
        _, to = message(i)
        halo_buf[to] = feats[send_ids[0, to]]
        return carry

    lax.fori_loop(0, n, gather, 0)
    pl.semaphore_wait(barrier, n - 1)

    def halo_copy(to):
        return pltpu.make_async_remote_copy(
            halo_buf.at[to], halo_in.at[me], halo_ss, halo_rs, device_id=(to,), device_id_type=MESH
        )

    def push_copy(to):
        return pltpu.make_async_remote_copy(
            push_buf.at[to], push_in.at[me], push_ss, push_rs, device_id=(to,), device_id_type=MESH
        )

    def dst_copy(to):
        return pltpu.make_async_remote_copy(
            dst_buf, dst_in.at[me], dst_ss, dst_rs, device_id=(to,), device_id_type=MESH
        )

    def first(i, carry):
        mask, to = message(i)

        @pl.when(mask > 0)
        def _():
            halo_copy(to).start()
            dst_copy(to).start()

        push_buf[to] = jnp.dot(
            push_tiles[to], feats[push_ids[0, to]], preferred_element_type=jnp.float32
        ).astype(jnp.bfloat16)
        return carry

    lax.fori_loop(0, n, first, 0)

    def second(i, carry):
        mask, to = message(i)

        @pl.when(mask > 0)
        def _():
            push_copy(to).start()

        return carry

    lax.fori_loop(0, n, second, 0)
    own = (
        pltpu.make_async_copy(halo_buf.at[me], halo_in.at[me], own_sems.at[0]),
        pltpu.make_async_copy(push_buf.at[me], push_in.at[me], own_sems.at[1]),
        pltpu.make_async_copy(dst_buf, dst_in.at[me], own_sems.at[2]),
    )
    for copy in own:
        copy.start()

    load_tiles.wait()
    slots = local_tiles.shape[1]

    def local(b, carry):
        total = jnp.zeros(feats.shape[1:], jnp.float32)
        for j in range(slots):
            live = jnp.minimum(jnp.maximum(local_cnt[b] - j, 0), 1).astype(jnp.float32)
            tile = tile_buf[b, j] * jnp.full((blk, blk), live, jnp.float32).astype(jnp.bfloat16)
            total += jnp.dot(tile, feats[local_ids[j, b]], preferred_element_type=jnp.float32)
        rows = pl.ds(pl.multiple_of(b * blk, blk), blk)
        local_buf[rows, :] = total
        base_buf[rows, :] = (
            jnp.dot(feats[b], w_self[...], preferred_element_type=jnp.float32) + bias[...]
        )
        return carry

    lax.fori_loop(0, feats.shape[0], local, 0)
    outs = (
        pltpu.make_async_copy(local_buf, local_out, out_sems.at[0]),
        pltpu.make_async_copy(base_buf, base_out, out_sems.at[1]),
    )
    for copy in outs:
        copy.start()
    for copy in own + outs:
        copy.wait()
    for buf, sem in (
        (halo_in, halo_rs),
        (push_in, push_rs),
        (dst_in, dst_rs),
        (halo_buf, halo_ss),
        (push_buf, push_ss),
        (dst_in, dst_ss),
    ):
        part = buf.at[pl.ds(0, n - 1)]
        pltpu.make_async_copy(part, part, sem).wait()


def exchange(n, send_ids, push_ids, local_ids, local_cnt, feats, push_tiles, local_tiles, w_self, bias, push_dst):
    blocks, blk, width = feats.shape
    smem = pl.BlockSpec(memory_space=pltpu.SMEM)
    vmem = pl.BlockSpec(memory_space=pltpu.VMEM)
    hbm = pl.BlockSpec(memory_space=pl.ANY)
    dma = pltpu.SemaphoreType.DMA
    return pl.pallas_call(
        functools.partial(exchange_kernel, n),
        out_shape=(
            jax.ShapeDtypeStruct((n, blk, width), jnp.bfloat16),
            jax.ShapeDtypeStruct((n, blk, width), jnp.bfloat16),
            jax.ShapeDtypeStruct((n, 1, max(n, 128)), jnp.int32),
            jax.ShapeDtypeStruct((blocks * blk, width), jnp.float32),
            jax.ShapeDtypeStruct((blocks * blk, width), jnp.float32),
        ),
        in_specs=[smem] * 4 + [vmem] * 2 + [hbm] + [vmem] * 3,
        out_specs=(hbm,) * 5,
        scratch_shapes=[
            pltpu.VMEM((n, blk, width), jnp.bfloat16),
            pltpu.VMEM((n, blk, width), jnp.bfloat16),
            pltpu.VMEM((blocks * blk, width), jnp.float32),
            pltpu.VMEM((blocks * blk, width), jnp.float32),
            pltpu.VMEM((1, max(n, 128)), jnp.int32),
            pltpu.VMEM(local_tiles.shape, jnp.bfloat16),
        ]
        + [dma] * 6
        + [dma((3,)), dma((3,))],
        compiler_params=pltpu.CompilerParams(
            collective_id=0, has_side_effects=True, vmem_limit_bytes=VMEM_BYTES
        ),
        name="exchange",
    )(send_ids, push_ids, local_ids, local_cnt, feats, push_tiles, local_tiles, w_self, bias, push_dst)


def dense_kernel(
    steps,
    group,
    halo_dst,
    push_dst,
    halo_in,
    halo_tiles,
    push_in,
    local_part,
    base,
    feats,
    cot,
    w_neigh,
    hidden,
    grads,
    gbias,
    acc,
    gt,
    gb,
):
    i = pl.program_id(0)
    me = lax.axis_index("dom")
    blk = halo_in.shape[1]
    rows, width = feats.shape

    @pl.when(i == 0)
    def _():
        acc[...] = jnp.zeros_like(acc)
        gt[...] = jnp.zeros_like(gt)
        gb[...] = jnp.zeros_like(gb)

    @pl.when(i < steps)
    def _():
        for k in range(group):
            q = i * group + k
            at = pl.ds(pl.multiple_of(halo_dst[q] * blk, blk), blk)
            acc[at, :] += jnp.dot(halo_tiles[k], halo_in[k], preferred_element_type=jnp.float32)
            at = pl.ds(pl.multiple_of(push_dst[q, 0, me] * blk, blk), blk)
            acc[at, :] += push_in[k].astype(jnp.float32)

    @pl.when(i >= steps)
    def _():
        at = pl.ds(pl.multiple_of((i - steps) * rows, rows), rows)
        agg = (acc[at, :] + local_part[...]).astype(jnp.bfloat16)
        pre = base[...] + jnp.dot(agg, w_neigh[...], preferred_element_type=jnp.float32)
        sigma = jax.nn.sigmoid(pre)
        hidden[...] = (pre * sigma).astype(jnp.bfloat16)
        dpre = (cot[...].astype(jnp.float32) * sigma * (1.0 + pre * (1.0 - sigma))).astype(
            jnp.bfloat16
        )
        gb[...] += jnp.sum(dpre.astype(jnp.float32).reshape(rows // 8, 8, width), axis=0)
        turned = dpre.T
        gt[0] += jnp.dot(turned, feats[...], preferred_element_type=jnp.float32)
        gt[1] += jnp.dot(turned, agg, preferred_element_type=jnp.float32)

    @pl.when(i == pl.num_programs(0) - 1)
    def _():
        grads[pl.ds(0, width), :] = gt[0].T
        grads[pl.ds(width, width), :] = gt[1].T
        gbias[...] = jnp.broadcast_to(jnp.sum(gb[...], axis=0, keepdims=True), gbias.shape)


def dense(halo_dst, push_dst, halo_in, halo_tiles, push_in, local_part, base, feats, cot, w_neigh):
    n, blk, width = halo_in.shape
    nodes = feats.shape[0]
    group, rows = 4, 512
    steps, chunks = n // group, nodes // rows

    def owners(i, *_):
        return (jnp.minimum(i, steps - 1), 0, 0)

    def nodes_at(i, *_):
        return (jnp.maximum(i - steps, 0), 0)

    arrived = pl.BlockSpec((group, blk, width), owners)
    chunk = pl.BlockSpec((rows, width), nodes_at)

    def whole(i, *_):
        return (0, 0)

    return pl.pallas_call(
        functools.partial(dense_kernel, steps, group),
        out_shape=(
            jax.ShapeDtypeStruct((nodes, width), jnp.bfloat16),
            jax.ShapeDtypeStruct((2 * width, width), jnp.float32),
            jax.ShapeDtypeStruct((8, width), jnp.float32),
        ),
        grid_spec=pltpu.PrefetchScalarGridSpec(
            num_scalar_prefetch=2,
            grid=(steps + chunks,),
            in_specs=[
                arrived,
                pl.BlockSpec((group, blk, blk), owners),
                arrived,
                chunk,
                chunk,
                chunk,
                chunk,
                pl.BlockSpec((width, width), whole),
            ],
            out_specs=(
                chunk,
                pl.BlockSpec((2 * width, width), whole),
                pl.BlockSpec((8, width), whole),
            ),
            scratch_shapes=[
                pltpu.VMEM((nodes, width), jnp.float32),
                pltpu.VMEM((2, width, width), jnp.float32),
                pltpu.VMEM((8, width), jnp.float32),
            ],
        ),
        compiler_params=pltpu.CompilerParams(
            dimension_semantics=("arbitrary",), vmem_limit_bytes=VMEM_BYTES
        ),
        name="dense",
    )(halo_dst, push_dst, halo_in, halo_tiles, push_in, local_part, base, feats, cot, w_neigh)


def reduce_kernel(
    n, term, gbias, out, bias_out, acc, send_buf, recv_buf, bias_in, ss, rs, gs, gr, bs, br, own
):
    me = lax.axis_index("dom")
    barrier = greet_all(n, me)
    size = term.shape[0]
    core, second, third = me % 2, (me // 2) % 2, (me // 4) % 2
    bits = [core, second * (1 - core) + third * core, third * (1 - core) + second * core]
    weights = [1, 2 + 2 * core, 4 - 2 * core]
    weight = 8
    while weight < n:
        bits.append((me // weight) % 2)
        weights.append(weight)
        weight *= 2
    partners = [me + (1 - 2 * bit) * w for bit, w in zip(bits, weights)]

    def bias_copy(to):
        return pltpu.make_async_remote_copy(
            gbias, bias_in.at[me], bs, br, device_id=(to,), device_id_type=MESH
        )

    own_bias = pltpu.make_async_copy(gbias, bias_in.at[me], own)
    own_bias.start()
    half = size // 2
    away = pl.multiple_of((1 - bits[0]) * half, half)
    send_buf[pl.ds(0, half), :] = term[pl.ds(away, half), :].astype(jnp.bfloat16)
    pl.semaphore_wait(barrier, n - 1)

    base = 0
    lo = 0
    for step, (bit, partner) in enumerate(zip(bits, partners)):
        half = size // 2
        copy = pltpu.make_async_remote_copy(
            send_buf.at[pl.ds(base, half)],
            recv_buf.at[pl.ds(base, half)],
            ss.at[step],
            rs.at[step],
            device_id=(partner,),
            device_id_type=MESH,
        )
        copy.start()
        if step == 0:

            def greet(i, carry):
                bias_copy(lax.rem(me + i, n)).start()
                return carry

            lax.fori_loop(1, n, greet, 0)
        lo = lo + bit * half
        source = term if step == 0 else acc
        copy.wait()
        if step + 1 < len(bits):
            nxt = half // 2
            bit2 = bits[step + 1]
            away = (1 - bit2) * nxt
            at = pl.multiple_of(lo + away, nxt)
            rel = pl.multiple_of(away, nxt)
            send_buf[pl.ds(base + half, nxt), :] = (
                source[pl.ds(at, nxt), :]
                + recv_buf[pl.ds(pl.multiple_of(base + rel, nxt), nxt), :].astype(jnp.float32)
            ).astype(jnp.bfloat16)
            keep = bit2 * nxt
            at = pl.multiple_of(lo + keep, nxt)
            acc[pl.ds(at, nxt), :] = source[pl.ds(at, nxt), :] + recv_buf[
                pl.ds(pl.multiple_of(base + keep, nxt), nxt), :
            ].astype(jnp.float32)
        else:
            at = pl.multiple_of(lo, half)
            out[pl.ds(at, half), :] = (
                source[pl.ds(at, half), :] + recv_buf[pl.ds(base, half), :].astype(jnp.float32)
            ).astype(jnp.bfloat16)
        base += half
        size = half

    own_bias.wait()
    part = bias_in.at[pl.ds(0, n - 1)]
    pltpu.make_async_copy(part, part, br).wait()
    bias_out[...] = jnp.sum(bias_in[...], axis=0)

    for step in reversed(range(len(bits))):
        at = pl.ds(pl.multiple_of(lo, size), size)
        copy = pltpu.make_async_remote_copy(
            out.at[at],
            out.at[at],
            gs.at[step],
            gr.at[step],
            device_id=(partners[step],),
            device_id_type=MESH,
        )
        copy.start()
        copy.wait()
        lo = lo - bits[step] * size
        size *= 2
    part = bias_in.at[pl.ds(0, n - 1)]
    pltpu.make_async_copy(part, part, bs).wait()


def reduce(n, term, gbias):
    size, width = term.shape
    steps = n.bit_length() - 1
    vmem = pl.BlockSpec(memory_space=pltpu.VMEM)
    dma = pltpu.SemaphoreType.DMA
    return pl.pallas_call(
        functools.partial(reduce_kernel, n),
        out_shape=(
            jax.ShapeDtypeStruct((size, width), jnp.bfloat16),
            jax.ShapeDtypeStruct(gbias.shape, jnp.float32),
        ),
        in_specs=[vmem, vmem],
        out_specs=(vmem, vmem),
        scratch_shapes=[
            pltpu.VMEM((size, width), jnp.float32),
            pltpu.VMEM((size, width), jnp.bfloat16),
            pltpu.VMEM((size, width), jnp.bfloat16),
            pltpu.VMEM((n,) + gbias.shape, jnp.float32),
            dma((steps,)),
            dma((steps,)),
            dma((steps,)),
            dma((steps,)),
            dma,
            dma,
            dma,
        ],
        compiler_params=pltpu.CompilerParams(
            collective_id=1, has_side_effects=True, vmem_limit_bytes=VMEM_BYTES
        ),
        name="reduce_grads",
    )(term, gbias)


def widen_kernel(grads, gbias, grad_self, grad_neigh, grad_bias):
    width = grad_self.shape[0]
    grad_self[...] = grads[pl.ds(0, width), :].astype(jnp.float32)
    grad_neigh[...] = grads[pl.ds(width, width), :].astype(jnp.float32)
    grad_bias[...] = gbias[pl.ds(0, 1), :]


def widen(grads, gbias):
    vmem = pl.BlockSpec(memory_space=pltpu.VMEM)
    out = jax.ShapeDtypeStruct((grads.shape[0] // 2, grads.shape[1]), jnp.float32)
    return pl.pallas_call(
        widen_kernel,
        out_shape=(out, out, jax.ShapeDtypeStruct((1, grads.shape[1]), jnp.float32)),
        in_specs=[vmem, vmem],
        out_specs=(vmem,) * 3,
        name="widen",
    )(grads, gbias)


def shards(
    n,
    feats,
    w_self,
    w_neigh,
    bias,
    local_tiles,
    local_src,
    local_cnt,
    halo_send,
    halo_dst,
    halo_tiles,
    push_src,
    push_dst,
    push_tiles,
    cotangent,
):
    width = feats.shape[1]
    halo_in, push_in, dst_in, local_part, base = exchange(
        n,
        halo_send,
        push_src,
        local_src.T,
        local_cnt,
        feats.reshape(-1, push_tiles.shape[2], width),
        push_tiles[0],
        local_tiles,
        w_self,
        bias[None, :],
        push_dst,
    )
    hidden_out, term, term_bias = dense(
        halo_dst[0],
        dst_in,
        halo_in,
        halo_tiles[0],
        push_in,
        local_part,
        base,
        feats,
        cotangent,
        w_neigh,
    )
    grads, gbias = reduce(n, term, term_bias)
    grad_self, grad_neigh, grad_bias = widen(grads, gbias)
    return (hidden_out, grad_self, grad_neigh, grad_bias.reshape(width))


def solution(mesh):
    placed = (
        P("dom", None),
        P(),
        P(),
        P(),
        P("dom", None, None, None),
        P("dom", None),
        P("dom"),
        P("dom", None),
        P("dom", None),
        P("dom", None, None, None),
        P("dom", None),
        P("dom", None),
        P("dom", None, None, None),
        P("dom", None),
    )
    return jax.shard_map(
        functools.partial(shards, mesh.shape["dom"]),
        mesh=mesh,
        in_specs=placed,
        out_specs=(P("dom", None), P(), P(), P()),
        check_vma=False,
    )
```

```python
import functools

import jax
import jax.numpy as jnp
from jax import lax
from jax.experimental import pallas as pl
from jax.experimental.pallas import tpu as pltpu
from jax.sharding import PartitionSpec as P

MESH = pl.DeviceIdType.MESH
VMEM_BYTES = 66_000_000
PLANE = 8


def flip(me, mask, n):
    out = 0
    weight = 1
    while weight < n:
        out = out + weight * ((me // weight + mask // weight) % 2)
        weight *= 2
    return out


def greet_all(n, me):
    barrier = pltpu.get_barrier_semaphore()

    def greet(i, carry):
        pl.semaphore_signal(
            barrier, inc=1, device_id=(lax.rem(me + i, n),), device_id_type=MESH
        )
        return carry

    lax.fori_loop(1, n, greet, 0)
    return barrier


def exchange_kernel(
    n,
    send_ids,
    push_ids,
    local_ids,
    local_cnt,
    feats,
    push_tiles,
    local_tiles,
    w_self,
    bias,
    push_dst,
    halo_in,
    push_in,
    dst_in,
    local_out,
    base_out,
    halo_buf,
    push_buf,
    local_buf,
    base_buf,
    dst_buf,
    tile_buf,
    halo_ss,
    halo_rs,
    push_ss,
    push_rs,
    dst_ss,
    dst_rs,
    own_sems,
    out_sems,
):
    me = lax.axis_index("dom")
    blk = push_tiles.shape[1]
    planes = n // PLANE
    barrier = greet_all(n, me)
    load_tiles = pltpu.make_async_copy(local_tiles, tile_buf, out_sems.at[2])
    load_tiles.start()
    dst_buf[...] = jnp.zeros_like(dst_buf)
    dst_buf[:, pl.ds(0, n)] = push_dst[...]

    def message(i):
        mask = ((i % planes + 1) % planes) * PLANE + i // planes
        return mask, flip(me, mask, n)

    def gather(i, carry):
        _, to = message(i)
        halo_buf[to] = feats[send_ids[0, to]]
        return carry

    lax.fori_loop(0, n, gather, 0)
    pl.semaphore_wait(barrier, n - 1)

    def halo_copy(to):
        return pltpu.make_async_remote_copy(
            halo_buf.at[to], halo_in.at[me], halo_ss, halo_rs, device_id=(to,), device_id_type=MESH
        )

    def push_copy(to):
        return pltpu.make_async_remote_copy(
            push_buf.at[to], push_in.at[me], push_ss, push_rs, device_id=(to,), device_id_type=MESH
        )

    def dst_copy(to):
        return pltpu.make_async_remote_copy(
            dst_buf, dst_in.at[me], dst_ss, dst_rs, device_id=(to,), device_id_type=MESH
        )

    def first(i, carry):
        mask, to = message(i)

        @pl.when(mask > 0)
        def _():
            halo_copy(to).start()
            dst_copy(to).start()

        push_buf[to] = jnp.dot(
            push_tiles[to], feats[push_ids[0, to]], preferred_element_type=jnp.float32
        ).astype(jnp.bfloat16)
        return carry

    lax.fori_loop(0, n, first, 0)

    def second(i, carry):
        mask, to = message(i)

        @pl.when(mask > 0)
        def _():
            push_copy(to).start()

        return carry

    lax.fori_loop(0, n, second, 0)
    own = (
        pltpu.make_async_copy(halo_buf.at[me], halo_in.at[me], own_sems.at[0]),
        pltpu.make_async_copy(push_buf.at[me], push_in.at[me], own_sems.at[1]),
        pltpu.make_async_copy(dst_buf, dst_in.at[me], own_sems.at[2]),
    )
    for copy in own:
        copy.start()

    load_tiles.wait()
    slots = local_tiles.shape[1]

    def local(b, carry):
        total = jnp.zeros(feats.shape[1:], jnp.float32)
        for j in range(slots):
            live = jnp.minimum(jnp.maximum(local_cnt[b] - j, 0), 1).astype(jnp.float32)
            tile = tile_buf[b, j] * jnp.full((blk, blk), live, jnp.float32).astype(jnp.bfloat16)
            total += jnp.dot(tile, feats[local_ids[j, b]], preferred_element_type=jnp.float32)
        rows = pl.ds(pl.multiple_of(b * blk, blk), blk)
        local_buf[rows, :] = total
        base_buf[rows, :] = (
            jnp.dot(feats[b], w_self[...], preferred_element_type=jnp.float32) + bias[...]
        )
        return carry

    lax.fori_loop(0, feats.shape[0], local, 0)
    outs = (
        pltpu.make_async_copy(local_buf, local_out, out_sems.at[0]),
        pltpu.make_async_copy(base_buf, base_out, out_sems.at[1]),
    )
    for copy in outs:
        copy.start()
    for copy in own + outs:
        copy.wait()
    for buf, sem in (
        (halo_in, halo_rs),
        (push_in, push_rs),
        (dst_in, dst_rs),
        (halo_buf, halo_ss),
        (push_buf, push_ss),
        (dst_in, dst_ss),
    ):
        part = buf.at[pl.ds(0, n - 1)]
        pltpu.make_async_copy(part, part, sem).wait()


def exchange(n, send_ids, push_ids, local_ids, local_cnt, feats, push_tiles, local_tiles, w_self, bias, push_dst):
    blocks, blk, width = feats.shape
    smem = pl.BlockSpec(memory_space=pltpu.SMEM)
    vmem = pl.BlockSpec(memory_space=pltpu.VMEM)
    hbm = pl.BlockSpec(memory_space=pl.ANY)
    dma = pltpu.SemaphoreType.DMA
    return pl.pallas_call(
        functools.partial(exchange_kernel, n),
        out_shape=(
            jax.ShapeDtypeStruct((n, blk, width), jnp.bfloat16),
            jax.ShapeDtypeStruct((n, blk, width), jnp.bfloat16),
            jax.ShapeDtypeStruct((n, 1, max(n, 128)), jnp.int32),
            jax.ShapeDtypeStruct((blocks * blk, width), jnp.float32),
            jax.ShapeDtypeStruct((blocks * blk, width), jnp.float32),
        ),
        in_specs=[smem] * 4 + [vmem] * 2 + [hbm] + [vmem] * 3,
        out_specs=(hbm,) * 5,
        scratch_shapes=[
            pltpu.VMEM((n, blk, width), jnp.bfloat16),
            pltpu.VMEM((n, blk, width), jnp.bfloat16),
            pltpu.VMEM((blocks * blk, width), jnp.float32),
            pltpu.VMEM((blocks * blk, width), jnp.float32),
            pltpu.VMEM((1, max(n, 128)), jnp.int32),
            pltpu.VMEM(local_tiles.shape, jnp.bfloat16),
        ]
        + [dma] * 6
        + [dma((3,)), dma((3,))],
        compiler_params=pltpu.CompilerParams(
            collective_id=0, has_side_effects=True, vmem_limit_bytes=VMEM_BYTES
        ),
        name="exchange",
    )(send_ids, push_ids, local_ids, local_cnt, feats, push_tiles, local_tiles, w_self, bias, push_dst)


def dense_kernel(
    steps,
    group,
    halo_dst,
    push_dst,
    halo_in,
    halo_tiles,
    push_in,
    local_part,
    base,
    feats,
    cot,
    w_neigh,
    hidden,
    grads,
    gbias,
    acc,
    gt,
    gb,
    agg_buf,
    dpre_buf,
):
    i = pl.program_id(0)
    me = lax.axis_index("dom")
    blk = halo_in.shape[1]
    rows, width = feats.shape

    @pl.when(i == 0)
    def _():
        acc[...] = jnp.zeros_like(acc)
        gt[...] = jnp.zeros_like(gt)
        gb[...] = jnp.zeros_like(gb)

    @pl.when(i < steps)
    def _():
        for k in range(group):
            q = i * group + k
            at = pl.ds(pl.multiple_of(halo_dst[q] * blk, blk), blk)
            acc[at, :] += jnp.dot(halo_tiles[k], halo_in[k], preferred_element_type=jnp.float32)
            at = pl.ds(pl.multiple_of(push_dst[q, 0, me] * blk, blk), blk)
            acc[at, :] += push_in[k].astype(jnp.float32)

    def gradients():
        turned = dpre_buf[...].T
        gt[0] += jnp.dot(turned, feats[...], preferred_element_type=jnp.float32)
        gt[1] += jnp.dot(turned, agg_buf[...], preferred_element_type=jnp.float32)

    def layer():
        at = pl.ds(pl.multiple_of((i - steps) * rows, rows), rows)
        agg = (acc[at, :] + local_part[...]).astype(jnp.bfloat16)
        pre = base[...] + jnp.dot(agg, w_neigh[...], preferred_element_type=jnp.float32)
        sigma = jax.nn.sigmoid(pre)
        hidden[...] = (pre * sigma).astype(jnp.bfloat16)
        dpre = (cot[...].astype(jnp.float32) * sigma * (1.0 + pre * (1.0 - sigma))).astype(
            jnp.bfloat16
        )
        gb[...] += jnp.sum(dpre.astype(jnp.float32).reshape(rows // 8, 8, width), axis=0)
        agg_buf[...] = agg
        dpre_buf[...] = dpre

    last = pl.num_programs(0) - 1
    pl.when(i == steps)(layer)

    @pl.when(jnp.logical_and(i > steps, i < last))
    def _():
        gradients()
        layer()

    pl.when(i == last)(gradients)

    @pl.when(i == pl.num_programs(0) - 1)
    def _():
        grads[pl.ds(0, width), :] = gt[0].T
        grads[pl.ds(width, width), :] = gt[1].T
        gbias[...] = jnp.broadcast_to(jnp.sum(gb[...], axis=0, keepdims=True), gbias.shape)


def dense(halo_dst, push_dst, halo_in, halo_tiles, push_in, local_part, base, feats, cot, w_neigh):
    n, blk, width = halo_in.shape
    nodes = feats.shape[0]
    group, rows = 4, 512
    steps, chunks = n // group, nodes // rows

    def owners(i, *_):
        return (jnp.minimum(i, steps - 1), 0, 0)

    def nodes_at(i, *_):
        return (jnp.clip(i - steps, 0, chunks - 1), 0)

    def nodes_before(i, *_):
        return (jnp.maximum(i - steps - 1, 0), 0)

    arrived = pl.BlockSpec((group, blk, width), owners)
    chunk = pl.BlockSpec((rows, width), nodes_at)

    def whole(i, *_):
        return (0, 0)

    return pl.pallas_call(
        functools.partial(dense_kernel, steps, group),
        out_shape=(
            jax.ShapeDtypeStruct((nodes, width), jnp.bfloat16),
            jax.ShapeDtypeStruct((2 * width, width), jnp.float32),
            jax.ShapeDtypeStruct((8, width), jnp.float32),
        ),
        grid_spec=pltpu.PrefetchScalarGridSpec(
            num_scalar_prefetch=2,
            grid=(steps + chunks + 1,),
            in_specs=[
                arrived,
                pl.BlockSpec((group, blk, blk), owners),
                arrived,
                chunk,
                chunk,
                pl.BlockSpec((rows, width), nodes_before),
                chunk,
                pl.BlockSpec((width, width), whole),
            ],
            out_specs=(
                chunk,
                pl.BlockSpec((2 * width, width), whole),
                pl.BlockSpec((8, width), whole),
            ),
            scratch_shapes=[
                pltpu.VMEM((nodes, width), jnp.float32),
                pltpu.VMEM((2, width, width), jnp.float32),
                pltpu.VMEM((8, width), jnp.float32),
                pltpu.VMEM((rows, width), jnp.bfloat16),
                pltpu.VMEM((rows, width), jnp.bfloat16),
            ],
        ),
        compiler_params=pltpu.CompilerParams(
            dimension_semantics=("arbitrary",), vmem_limit_bytes=VMEM_BYTES
        ),
        name="dense",
    )(halo_dst, push_dst, halo_in, halo_tiles, push_in, local_part, base, feats, cot, w_neigh)


def reduce_kernel(n, term, gbias, out, bias_out, acc, send_buf, recv_buf, bias_in, ss, rs, bs, br, own):
    me = lax.axis_index("dom")
    barrier = greet_all(n, me)
    parts, size, cols = out.shape
    planes = n // PLANE
    plane, place = me // PLANE, me % PLANE
    core, second, third = me % 2, (me // 2) % 2, (me // 4) % 2
    bits = [core, second * (1 - core) + third * core, third * (1 - core) + second * core]
    weights = [1, 2 + 2 * core, 4 - 2 * core]
    partners = [me + (1 - 2 * bit) * w for bit, w in zip(bits, weights)]
    steps = len(bits)
    sizes = [size // 2 ** (k + 1) for k in range(steps)]
    bases = [size - 2 * s for s in sizes]
    starts = [0]
    for bit, s in zip(bits, sizes):
        starts.append(starts[-1] + bit * s)

    def bias_copy(to):
        return pltpu.make_async_remote_copy(
            gbias, bias_in.at[me], bs, br, device_id=(to,), device_id_type=MESH
        )

    def remote(src, dst, p, k, to):
        return pltpu.make_async_remote_copy(
            src, dst, ss.at[p, k], rs.at[p, k], device_id=(to,), device_id_type=MESH
        )

    def halving(p, k):
        rows = pl.ds(bases[k], sizes[k])
        return remote(send_buf.at[p, rows], recv_buf.at[p, rows], p, k, partners[k])

    def value(p, k, off, count):
        at = pl.ds(pl.multiple_of(starts[k] + off, count), count)
        if k <= 1:
            mine = term[at, pl.ds(p * cols, cols)]
        else:
            mine = acc[p, at, :]
        if k == 0:
            return mine
        got = pl.ds(pl.multiple_of(bases[k - 1] + off, count), count)
        return mine + recv_buf[p, got, :].astype(jnp.float32)

    def prepare(p, k):
        half = sizes[k]
        send_buf[p, pl.ds(bases[k], half), :] = value(p, k, (1 - bits[k]) * half, half).astype(
            jnp.bfloat16
        )
        if k > 0:
            at = pl.ds(pl.multiple_of(starts[k + 1], half), half)
            acc[p, at, :] = value(p, k, bits[k] * half, half)

    own_bias = pltpu.make_async_copy(gbias, bias_in.at[me], own)
    own_bias.start()
    for p in range(parts):
        prepare(p, 0)
    pl.semaphore_wait(barrier, n - 1)
    for p in range(parts):
        halving(p, 0).start()

    def greet(i, carry):
        bias_copy(lax.rem(me + i, n)).start()
        return carry

    lax.fori_loop(1, n, greet, 0)
    for k in range(1, steps):
        for p in range(parts):
            halving(p, k - 1).wait()
            prepare(p, k)
            halving(p, k).start()

    held, lo, last = sizes[-1], starts[-1], bases[-1] + sizes[-1]
    piece = held // planes

    def scatter(p, h):
        to = lax.rem(plane + h, planes)
        src = pl.ds(pl.multiple_of(last + to * piece, piece), piece)
        dst = pl.ds(pl.multiple_of(last + plane * piece, piece), piece)
        return remote(send_buf.at[p, src], recv_buf.at[p, dst], p, steps + h - 1, to * PLANE + place)

    for p in range(parts):
        halving(p, steps - 1).wait()
        full = value(p, steps, 0, held)
        send_buf[p, pl.ds(last, held), :] = full.astype(jnp.bfloat16)
        acc[p, pl.ds(pl.multiple_of(lo, held), held), :] = full
        for h in range(1, planes):
            scatter(p, h).start()

    mine = pl.ds(pl.multiple_of(lo + plane * piece, piece), piece)

    def spread(p, h):
        to = lax.rem(plane + h, planes) * PLANE + place
        return remote(out.at[p, mine], out.at[p, mine], p, steps + planes - 2 + h, to)

    for p in range(parts):
        total = acc[p, mine, :]
        for h in range(1, planes):
            scatter(p, h).wait()
        for h in range(1, planes):
            slot = last + lax.rem(plane + planes - h, planes) * piece
            total += recv_buf[p, pl.ds(pl.multiple_of(slot, piece), piece), :].astype(jnp.float32)
        out[p, mine, :] = total.astype(jnp.bfloat16)
        for h in range(1, planes):
            spread(p, h).start()

    own_bias.wait()
    part = bias_in.at[pl.ds(0, n - 1)]
    pltpu.make_async_copy(part, part, br).wait()
    bias_out[...] = jnp.sum(bias_in[...], axis=0)

    def doubling(p, k):
        at = pl.ds(pl.multiple_of(starts[k + 1], sizes[k]), sizes[k])
        return remote(out.at[p, at], out.at[p, at], p, 2 * (planes - 1) + steps + k, partners[k])

    for p in range(parts):
        for h in range(1, planes):
            spread(p, h).wait()
        doubling(p, steps - 1).start()
    for k in reversed(range(steps - 1)):
        for p in range(parts):
            doubling(p, k + 1).wait()
            doubling(p, k).start()
    for p in range(parts):
        doubling(p, 0).wait()
    pltpu.make_async_copy(part, part, bs).wait()


def reduce(n, term, gbias):
    size, width = term.shape
    parts = 2
    copies = 2 * (PLANE.bit_length() - 1 + n // PLANE - 1)
    vmem = pl.BlockSpec(memory_space=pltpu.VMEM)
    dma = pltpu.SemaphoreType.DMA
    split = (parts, size, width // parts)
    return pl.pallas_call(
        functools.partial(reduce_kernel, n),
        out_shape=(
            jax.ShapeDtypeStruct(split, jnp.bfloat16),
            jax.ShapeDtypeStruct(gbias.shape, jnp.float32),
        ),
        in_specs=[vmem, vmem],
        out_specs=(vmem, vmem),
        scratch_shapes=[
            pltpu.VMEM(split, jnp.float32),
            pltpu.VMEM(split, jnp.bfloat16),
            pltpu.VMEM(split, jnp.bfloat16),
            pltpu.VMEM((n,) + gbias.shape, jnp.float32),
            dma((parts, copies)),
            dma((parts, copies)),
            dma,
            dma,
            dma,
        ],
        compiler_params=pltpu.CompilerParams(
            collective_id=1, has_side_effects=True, vmem_limit_bytes=VMEM_BYTES
        ),
        name="reduce_grads",
    )(term, gbias)


def widen_kernel(grads, gbias, grad_self, grad_neigh, grad_bias):
    width = grad_self.shape[0]
    parts, _, cols = grads.shape
    for p in range(parts):
        at = pl.ds(p * cols, cols)
        grad_self[:, at] = grads[p, pl.ds(0, width), :].astype(jnp.float32)
        grad_neigh[:, at] = grads[p, pl.ds(width, width), :].astype(jnp.float32)
    grad_bias[...] = gbias[pl.ds(0, 1), :]


def widen(grads, gbias):
    vmem = pl.BlockSpec(memory_space=pltpu.VMEM)
    width = gbias.shape[1]
    out = jax.ShapeDtypeStruct((grads.shape[1] // 2, width), jnp.float32)
    return pl.pallas_call(
        widen_kernel,
        out_shape=(out, out, jax.ShapeDtypeStruct((1, width), jnp.float32)),
        in_specs=[vmem, vmem],
        out_specs=(vmem,) * 3,
        name="widen",
    )(grads, gbias)


def shards(
    n,
    feats,
    w_self,
    w_neigh,
    bias,
    local_tiles,
    local_src,
    local_cnt,
    halo_send,
    halo_dst,
    halo_tiles,
    push_src,
    push_dst,
    push_tiles,
    cotangent,
):
    width = feats.shape[1]
    halo_in, push_in, dst_in, local_part, base = exchange(
        n,
        halo_send,
        push_src,
        local_src.T,
        local_cnt,
        feats.reshape(-1, push_tiles.shape[2], width),
        push_tiles[0],
        local_tiles,
        w_self,
        bias[None, :],
        push_dst,
    )
    hidden_out, term, term_bias = dense(
        halo_dst[0],
        dst_in,
        halo_in,
        halo_tiles[0],
        push_in,
        local_part,
        base,
        feats,
        cotangent,
        w_neigh,
    )
    grads, gbias = reduce(n, term, term_bias)
    grad_self, grad_neigh, grad_bias = widen(grads, gbias)
    return (hidden_out, grad_self, grad_neigh, grad_bias.reshape(width))


def solution(mesh):
    placed = (
        P("dom", None),
        P(),
        P(),
        P(),
        P("dom", None, None, None),
        P("dom", None),
        P("dom"),
        P("dom", None),
        P("dom", None),
        P("dom", None, None, None),
        P("dom", None),
        P("dom", None),
        P("dom", None, None, None),
        P("dom", None),
    )
    return jax.shard_map(
        functools.partial(shards, mesh.shape["dom"]),
        mesh=mesh,
        in_specs=placed,
        out_specs=(P("dom", None), P(), P(), P()),
        check_vma=False,
    )
```

```python
import functools

import jax
import jax.numpy as jnp
from jax import lax
from jax.experimental import pallas as pl
from jax.experimental.pallas import tpu as pltpu
from jax.sharding import PartitionSpec as P

MESH = pl.DeviceIdType.MESH
VMEM_BYTES = 66_000_000
PLANE = 8


def flip(me, mask, n):
    out = 0
    weight = 1
    while weight < n:
        out = out + weight * ((me // weight + mask // weight) % 2)
        weight *= 2
    return out


def greet_all(n, me):
    barrier = pltpu.get_barrier_semaphore()

    def greet(i, carry):
        pl.semaphore_signal(
            barrier, inc=1, device_id=(lax.rem(me + i, n),), device_id_type=MESH
        )
        return carry

    lax.fori_loop(1, n, greet, 0)
    return barrier


def exchange_kernel(
    n,
    send_ids,
    push_ids,
    local_ids,
    local_cnt,
    feats,
    push_tiles,
    local_tiles,
    w_self,
    bias,
    push_dst,
    halo_in,
    push_in,
    dst_in,
    local_out,
    base_out,
    halo_buf,
    push_buf,
    local_buf,
    base_buf,
    dst_buf,
    tile_buf,
    halo_ss,
    halo_rs,
    push_ss,
    push_rs,
    dst_ss,
    dst_rs,
    own_sems,
    out_sems,
):
    me = lax.axis_index("dom")
    blk = push_tiles.shape[1]
    planes = n // PLANE
    barrier = greet_all(n, me)
    load_tiles = pltpu.make_async_copy(local_tiles, tile_buf, out_sems.at[2])
    load_tiles.start()
    dst_buf[...] = jnp.zeros_like(dst_buf)
    dst_buf[:, pl.ds(0, n)] = push_dst[...]

    def message(i):
        mask = ((i % planes + 1) % planes) * PLANE + i // planes
        return mask, flip(me, mask, n)

    def gather(i, carry):
        _, to = message(i)
        halo_buf[to] = feats[send_ids[0, to]]
        return carry

    lax.fori_loop(0, n, gather, 0)
    pl.semaphore_wait(barrier, n - 1)

    def halo_copy(to):
        return pltpu.make_async_remote_copy(
            halo_buf.at[to], halo_in.at[me], halo_ss, halo_rs, device_id=(to,), device_id_type=MESH
        )

    def push_copy(to):
        return pltpu.make_async_remote_copy(
            push_buf.at[to], push_in.at[me], push_ss, push_rs, device_id=(to,), device_id_type=MESH
        )

    def dst_copy(to):
        return pltpu.make_async_remote_copy(
            dst_buf, dst_in.at[me], dst_ss, dst_rs, device_id=(to,), device_id_type=MESH
        )

    def first(i, carry):
        mask, to = message(i)

        @pl.when(mask > 0)
        def _():
            halo_copy(to).start()
            dst_copy(to).start()

        push_buf[to] = jnp.dot(
            push_tiles[to], feats[push_ids[0, to]], preferred_element_type=jnp.float32
        ).astype(jnp.bfloat16)
        return carry

    lax.fori_loop(0, n, first, 0)

    def second(i, carry):
        mask, to = message(i)

        @pl.when(mask > 0)
        def _():
            push_copy(to).start()

        return carry

    lax.fori_loop(0, n, second, 0)
    own = (
        pltpu.make_async_copy(halo_buf.at[me], halo_in.at[me], own_sems.at[0]),
        pltpu.make_async_copy(push_buf.at[me], push_in.at[me], own_sems.at[1]),
        pltpu.make_async_copy(dst_buf, dst_in.at[me], own_sems.at[2]),
    )
    for copy in own:
        copy.start()

    load_tiles.wait()
    slots = local_tiles.shape[1]

    def local(b, carry):
        total = jnp.zeros(feats.shape[1:], jnp.float32)
        for j in range(slots):
            live = jnp.minimum(jnp.maximum(local_cnt[b] - j, 0), 1).astype(jnp.float32)
            tile = tile_buf[b, j] * jnp.full((blk, blk), live, jnp.float32).astype(jnp.bfloat16)
            total += jnp.dot(tile, feats[local_ids[j, b]], preferred_element_type=jnp.float32)
        rows = pl.ds(pl.multiple_of(b * blk, blk), blk)
        local_buf[rows, :] = total
        base_buf[rows, :] = (
            jnp.dot(feats[b], w_self[...], preferred_element_type=jnp.float32) + bias[...]
        )
        return carry

    lax.fori_loop(0, feats.shape[0], local, 0)
    outs = (
        pltpu.make_async_copy(local_buf, local_out, out_sems.at[0]),
        pltpu.make_async_copy(base_buf, base_out, out_sems.at[1]),
    )
    for copy in outs:
        copy.start()
    for copy in own + outs:
        copy.wait()
    for buf, sem in (
        (halo_in, halo_rs),
        (push_in, push_rs),
        (dst_in, dst_rs),
        (halo_buf, halo_ss),
        (push_buf, push_ss),
        (dst_in, dst_ss),
    ):
        part = buf.at[pl.ds(0, n - 1)]
        pltpu.make_async_copy(part, part, sem).wait()


def exchange(n, send_ids, push_ids, local_ids, local_cnt, feats, push_tiles, local_tiles, w_self, bias, push_dst):
    blocks, blk, width = feats.shape
    smem = pl.BlockSpec(memory_space=pltpu.SMEM)
    vmem = pl.BlockSpec(memory_space=pltpu.VMEM)
    hbm = pl.BlockSpec(memory_space=pl.ANY)
    dma = pltpu.SemaphoreType.DMA
    return pl.pallas_call(
        functools.partial(exchange_kernel, n),
        out_shape=(
            jax.ShapeDtypeStruct((n, blk, width), jnp.bfloat16),
            jax.ShapeDtypeStruct((n, blk, width), jnp.bfloat16),
            jax.ShapeDtypeStruct((n, 1, max(n, 128)), jnp.int32),
            jax.ShapeDtypeStruct((blocks * blk, width), jnp.float32),
            jax.ShapeDtypeStruct((blocks * blk, width), jnp.float32),
        ),
        in_specs=[smem] * 4 + [vmem] * 2 + [hbm] + [vmem] * 3,
        out_specs=(hbm,) * 5,
        scratch_shapes=[
            pltpu.VMEM((n, blk, width), jnp.bfloat16),
            pltpu.VMEM((n, blk, width), jnp.bfloat16),
            pltpu.VMEM((blocks * blk, width), jnp.float32),
            pltpu.VMEM((blocks * blk, width), jnp.float32),
            pltpu.VMEM((1, max(n, 128)), jnp.int32),
            pltpu.VMEM(local_tiles.shape, jnp.bfloat16),
        ]
        + [dma] * 6
        + [dma((3,)), dma((3,))],
        compiler_params=pltpu.CompilerParams(
            collective_id=0, has_side_effects=True, vmem_limit_bytes=VMEM_BYTES
        ),
        name="exchange",
    )(send_ids, push_ids, local_ids, local_cnt, feats, push_tiles, local_tiles, w_self, bias, push_dst)


def dense_kernel(
    steps,
    group,
    halo_dst,
    push_dst,
    halo_in,
    halo_tiles,
    push_in,
    local_part,
    base,
    feats,
    cot,
    w_neigh,
    hidden,
    grads,
    gbias,
    acc,
    gt,
    gb,
    agg_buf,
    dpre_buf,
):
    i = pl.program_id(0)
    me = lax.axis_index("dom")
    blk = halo_in.shape[1]
    rows, width = feats.shape

    @pl.when(i == 0)
    def _():
        acc[...] = jnp.zeros_like(acc)
        gt[...] = jnp.zeros_like(gt)
        gb[...] = jnp.zeros_like(gb)

    @pl.when(i < steps)
    def _():
        for k in range(group):
            q = i * group + k
            at = pl.ds(pl.multiple_of(halo_dst[q] * blk, blk), blk)
            acc[at, :] += jnp.dot(halo_tiles[k], halo_in[k], preferred_element_type=jnp.float32)
            at = pl.ds(pl.multiple_of(push_dst[q, 0, me] * blk, blk), blk)
            acc[at, :] += push_in[k].astype(jnp.float32)

    def gradients():
        turned = dpre_buf[...].T
        gt[0] += jnp.dot(turned, feats[...], preferred_element_type=jnp.float32)
        gt[1] += jnp.dot(turned, agg_buf[...], preferred_element_type=jnp.float32)

    def layer():
        at = pl.ds(pl.multiple_of((i - steps) * rows, rows), rows)
        agg = (acc[at, :] + local_part[...]).astype(jnp.bfloat16)
        pre = base[...] + jnp.dot(agg, w_neigh[...], preferred_element_type=jnp.float32)
        sigma = jax.nn.sigmoid(pre)
        hidden[...] = (pre * sigma).astype(jnp.bfloat16)
        dpre = (cot[...].astype(jnp.float32) * sigma * (1.0 + pre * (1.0 - sigma))).astype(
            jnp.bfloat16
        )
        gb[...] += jnp.sum(dpre.astype(jnp.float32).reshape(rows // 8, 8, width), axis=0)
        agg_buf[...] = agg
        dpre_buf[...] = dpre

    last = pl.num_programs(0) - 1
    pl.when(i == steps)(layer)

    @pl.when(jnp.logical_and(i > steps, i < last))
    def _():
        gradients()
        layer()

    pl.when(i == last)(gradients)

    @pl.when(i == pl.num_programs(0) - 1)
    def _():
        grads[pl.ds(0, width), :] = gt[0].T
        grads[pl.ds(width, width), :] = gt[1].T
        gbias[...] = jnp.broadcast_to(jnp.sum(gb[...], axis=0, keepdims=True), gbias.shape)


def dense(halo_dst, push_dst, halo_in, halo_tiles, push_in, local_part, base, feats, cot, w_neigh):
    n, blk, width = halo_in.shape
    nodes = feats.shape[0]
    group, rows = 8, 1024
    steps, chunks = n // group, nodes // rows

    def owners(i, *_):
        return (jnp.minimum(i, steps - 1), 0, 0)

    def nodes_at(i, *_):
        return (jnp.clip(i - steps, 0, chunks - 1), 0)

    def nodes_before(i, *_):
        return (jnp.maximum(i - steps - 1, 0), 0)

    arrived = pl.BlockSpec((group, blk, width), owners)
    chunk = pl.BlockSpec((rows, width), nodes_at)

    def whole(i, *_):
        return (0, 0)

    return pl.pallas_call(
        functools.partial(dense_kernel, steps, group),
        out_shape=(
            jax.ShapeDtypeStruct((nodes, width), jnp.bfloat16),
            jax.ShapeDtypeStruct((2 * width, width), jnp.float32),
            jax.ShapeDtypeStruct((8, width), jnp.float32),
        ),
        grid_spec=pltpu.PrefetchScalarGridSpec(
            num_scalar_prefetch=2,
            grid=(steps + chunks + 1,),
            in_specs=[
                arrived,
                pl.BlockSpec((group, blk, blk), owners),
                arrived,
                chunk,
                chunk,
                pl.BlockSpec((rows, width), nodes_before),
                chunk,
                pl.BlockSpec((width, width), whole),
            ],
            out_specs=(
                chunk,
                pl.BlockSpec((2 * width, width), whole),
                pl.BlockSpec((8, width), whole),
            ),
            scratch_shapes=[
                pltpu.VMEM((nodes, width), jnp.float32),
                pltpu.VMEM((2, width, width), jnp.float32),
                pltpu.VMEM((8, width), jnp.float32),
                pltpu.VMEM((rows, width), jnp.bfloat16),
                pltpu.VMEM((rows, width), jnp.bfloat16),
            ],
        ),
        compiler_params=pltpu.CompilerParams(
            dimension_semantics=("arbitrary",), vmem_limit_bytes=VMEM_BYTES
        ),
        name="dense",
    )(halo_dst, push_dst, halo_in, halo_tiles, push_in, local_part, base, feats, cot, w_neigh)


def reduce_kernel(n, term, gbias, out, bias_out, acc, send_buf, recv_buf, bias_in, ss, rs, bs, br, own):
    me = lax.axis_index("dom")
    barrier = greet_all(n, me)
    parts, size, cols = out.shape
    planes = n // PLANE
    plane, place = me // PLANE, me % PLANE
    core, second, third = me % 2, (me // 2) % 2, (me // 4) % 2
    bits = [core, second * (1 - core) + third * core, third * (1 - core) + second * core]
    weights = [1, 2 + 2 * core, 4 - 2 * core]
    partners = [me + (1 - 2 * bit) * w for bit, w in zip(bits, weights)]
    steps = len(bits)
    sizes = [size // 2 ** (k + 1) for k in range(steps)]
    bases = [size - 2 * s for s in sizes]
    starts = [0]
    for bit, s in zip(bits, sizes):
        starts.append(starts[-1] + bit * s)

    def bias_copy(to):
        return pltpu.make_async_remote_copy(
            gbias, bias_in.at[me], bs, br, device_id=(to,), device_id_type=MESH
        )

    def remote(src, dst, p, k, to):
        return pltpu.make_async_remote_copy(
            src, dst, ss.at[p, k], rs.at[p, k], device_id=(to,), device_id_type=MESH
        )

    def halving(p, k):
        rows = pl.ds(bases[k], sizes[k])
        return remote(send_buf.at[p, rows], recv_buf.at[p, rows], p, k, partners[k])

    def value(p, k, off, count):
        at = pl.ds(pl.multiple_of(starts[k] + off, count), count)
        if k <= 1:
            mine = term[at, pl.ds(p * cols, cols)]
        else:
            mine = acc[p, at, :]
        if k == 0:
            return mine
        got = pl.ds(pl.multiple_of(bases[k - 1] + off, count), count)
        return mine + recv_buf[p, got, :].astype(jnp.float32)

    def prepare(p, k):
        half = sizes[k]
        send_buf[p, pl.ds(bases[k], half), :] = value(p, k, (1 - bits[k]) * half, half).astype(
            jnp.bfloat16
        )
        if k > 0:
            at = pl.ds(pl.multiple_of(starts[k + 1], half), half)
            acc[p, at, :] = value(p, k, bits[k] * half, half)

    own_bias = pltpu.make_async_copy(gbias, bias_in.at[me], own)
    own_bias.start()
    for p in range(parts):
        prepare(p, 0)
    pl.semaphore_wait(barrier, n - 1)
    for p in range(parts):
        halving(p, 0).start()

    def greet(i, carry):
        bias_copy(lax.rem(me + i, n)).start()
        return carry

    lax.fori_loop(1, n, greet, 0)
    for k in range(1, steps):
        for p in range(parts):
            halving(p, k - 1).wait()
            prepare(p, k)
            halving(p, k).start()

    held, lo, last = sizes[-1], starts[-1], bases[-1] + sizes[-1]
    piece = held // planes

    def scatter(p, h):
        to = lax.rem(plane + h, planes)
        src = pl.ds(pl.multiple_of(last + to * piece, piece), piece)
        dst = pl.ds(pl.multiple_of(last + plane * piece, piece), piece)
        return remote(send_buf.at[p, src], recv_buf.at[p, dst], p, steps + h - 1, to * PLANE + place)

    for p in range(parts):
        halving(p, steps - 1).wait()
        full = value(p, steps, 0, held)
        send_buf[p, pl.ds(last, held), :] = full.astype(jnp.bfloat16)
        acc[p, pl.ds(pl.multiple_of(lo, held), held), :] = full
        for h in range(1, planes):
            scatter(p, h).start()

    mine = pl.ds(pl.multiple_of(lo + plane * piece, piece), piece)

    def spread(p, h):
        to = lax.rem(plane + h, planes) * PLANE + place
        return remote(out.at[p, mine], out.at[p, mine], p, steps + planes - 2 + h, to)

    for p in range(parts):
        total = acc[p, mine, :]
        for h in range(1, planes):
            scatter(p, h).wait()
        for h in range(1, planes):
            slot = last + lax.rem(plane + planes - h, planes) * piece
            total += recv_buf[p, pl.ds(pl.multiple_of(slot, piece), piece), :].astype(jnp.float32)
        out[p, mine, :] = total.astype(jnp.bfloat16)
        for h in range(1, planes):
            spread(p, h).start()

    own_bias.wait()
    part = bias_in.at[pl.ds(0, n - 1)]
    pltpu.make_async_copy(part, part, br).wait()
    bias_out[...] = jnp.sum(bias_in[...], axis=0)

    def doubling(p, k):
        at = pl.ds(pl.multiple_of(starts[k + 1], sizes[k]), sizes[k])
        return remote(out.at[p, at], out.at[p, at], p, 2 * (planes - 1) + steps + k, partners[k])

    for p in range(parts):
        for h in range(1, planes):
            spread(p, h).wait()
        doubling(p, steps - 1).start()
    for k in reversed(range(steps - 1)):
        for p in range(parts):
            doubling(p, k + 1).wait()
            doubling(p, k).start()
    for p in range(parts):
        doubling(p, 0).wait()
    pltpu.make_async_copy(part, part, bs).wait()


def reduce(n, term, gbias):
    size, width = term.shape
    parts = 4
    copies = 2 * (PLANE.bit_length() - 1 + n // PLANE - 1)
    vmem = pl.BlockSpec(memory_space=pltpu.VMEM)
    dma = pltpu.SemaphoreType.DMA
    split = (parts, size, width // parts)
    return pl.pallas_call(
        functools.partial(reduce_kernel, n),
        out_shape=(
            jax.ShapeDtypeStruct(split, jnp.bfloat16),
            jax.ShapeDtypeStruct(gbias.shape, jnp.float32),
        ),
        in_specs=[vmem, vmem],
        out_specs=(vmem, vmem),
        scratch_shapes=[
            pltpu.VMEM(split, jnp.float32),
            pltpu.VMEM(split, jnp.bfloat16),
            pltpu.VMEM(split, jnp.bfloat16),
            pltpu.VMEM((n,) + gbias.shape, jnp.float32),
            dma((parts, copies)),
            dma((parts, copies)),
            dma,
            dma,
            dma,
        ],
        compiler_params=pltpu.CompilerParams(
            collective_id=1, has_side_effects=True, vmem_limit_bytes=VMEM_BYTES
        ),
        name="reduce_grads",
    )(term, gbias)


def widen_kernel(grads, gbias, grad_self, grad_neigh, grad_bias):
    width = grad_self.shape[0]
    parts, _, cols = grads.shape
    for p in range(parts):
        at = pl.ds(p * cols, cols)
        grad_self[:, at] = grads[p, pl.ds(0, width), :].astype(jnp.float32)
        grad_neigh[:, at] = grads[p, pl.ds(width, width), :].astype(jnp.float32)
    grad_bias[...] = gbias[pl.ds(0, 1), :]


def widen(grads, gbias):
    vmem = pl.BlockSpec(memory_space=pltpu.VMEM)
    width = gbias.shape[1]
    out = jax.ShapeDtypeStruct((grads.shape[1] // 2, width), jnp.float32)
    return pl.pallas_call(
        widen_kernel,
        out_shape=(out, out, jax.ShapeDtypeStruct((1, width), jnp.float32)),
        in_specs=[vmem, vmem],
        out_specs=(vmem,) * 3,
        name="widen",
    )(grads, gbias)


def shards(
    n,
    feats,
    w_self,
    w_neigh,
    bias,
    local_tiles,
    local_src,
    local_cnt,
    halo_send,
    halo_dst,
    halo_tiles,
    push_src,
    push_dst,
    push_tiles,
    cotangent,
):
    width = feats.shape[1]
    halo_in, push_in, dst_in, local_part, base = exchange(
        n,
        halo_send,
        push_src,
        local_src.T,
        local_cnt,
        feats.reshape(-1, push_tiles.shape[2], width),
        push_tiles[0],
        local_tiles,
        w_self,
        bias[None, :],
        push_dst,
    )
    hidden_out, term, term_bias = dense(
        halo_dst[0],
        dst_in,
        halo_in,
        halo_tiles[0],
        push_in,
        local_part,
        base,
        feats,
        cotangent,
        w_neigh,
    )
    grads, gbias = reduce(n, term, term_bias)
    grad_self, grad_neigh, grad_bias = widen(grads, gbias)
    return (hidden_out, grad_self, grad_neigh, grad_bias.reshape(width))


def solution(mesh):
    placed = (
        P("dom", None),
        P(),
        P(),
        P(),
        P("dom", None, None, None),
        P("dom", None),
        P("dom"),
        P("dom", None),
        P("dom", None),
        P("dom", None, None, None),
        P("dom", None),
        P("dom", None),
        P("dom", None, None, None),
        P("dom", None),
    )
    return jax.shard_map(
        functools.partial(shards, mesh.shape["dom"]),
        mesh=mesh,
        in_specs=placed,
        out_specs=(P("dom", None), P(), P(), P()),
        check_vma=False,
    )
```
